512 devices in a mesh: pair: 16 (over y, z_lo), task: 32 (over z_hi, x, core).
Axes of the slice: x: 4, y: 4, z: 16 (z_hi: 4, z_lo: 4; z = z_hi * 4 + z_lo), core: 2. Of those that a mesh axis runs over, the one named last changes fastest.
Arguments:
- factor_blocks: bfloat16 [64, 1536, 625], P('task', 'pair'), may hold values from -1.25 to 1.25
- amplitudes: bfloat16 [64, 512, 625], P('task', 'pair'), may hold values from -0.15625 to 0.15625
- residual_in: float32 [64, 512, 625], P('task', 'pair'), may hold values from -6 to 6
- task_owners: int32 [512, 3], replicated, may hold values from 0 to 31, all different within a row; in each aligned block of 16 rows (0 to 15, 16 to 31, ...) at most 2 rows name the same one
- task_local: int32 [512, 4], replicated, may hold values from 0 to 1
Outputs:
- residual_out: float32 [64, 512, 625], P('task', 'pair')
The draws below stay inside these ranges and needn't reach their ends.
Inputs may be any that keep to these rules, and one draw needn't show every extreme that they name: `task_owners`: the three numbers of a row differ; in each aligned block of 16 rows no number appears more than 2 times.
All inputs are finite; a program needn't handle non-finite values.
Results may differ from the reference program's by a relative error of at most 0.012.
Values may be sent and summed in bfloat16 or wider, within the bound.
A program may use at most 64 MiB of HBM per device.

```python
import math
import jax
import jax.numpy as jnp
import numpy as np
from jax import lax

TV = 25
TT = 625
NAUX = 1536
NPAIR = 512
BLK_DEV = 2
MOST = 2
NBLK = 64
NTASK = 512
N_PAIR = 16
N_TASK = 32


def with_ends(array, rng, smallest, high):
    dims = array.shape
    spot = [jax.random.randint(jax.random.fold_in(rng, axis), (), 0, dims[axis]) for axis in range(len(dims))]
    array = array.at[tuple(spot)].set(smallest)
    longest = dims.index(max(dims))
    spot[longest] = (spot[longest] + 1) % dims[longest]
    return array.at[tuple(spot)].set(high)


def block_levels(key, shape, split, least, high):
    def one(axis_at, blocks):
        steps = jax.random.uniform(jax.random.fold_in(jax.random.fold_in(key, 6), axis_at), (blocks,), jnp.float32, least / len(split), high / len(split))
        return jnp.repeat(jnp.exp(steps), shape[axis_at] // blocks).reshape((-1,) + (1,) * (len(shape) - axis_at - 1))

    factor_of = one(*split[0])
    for cut in split[1:]:
        factor_of = factor_of * one(*cut)
    return factor_of


def shared_out(stream_key, own, number, rows, amount, top, bound, skew):
    order = jax.random.permutation(stream_key, amount)
    packed, ordinary = shares(amount, rows * top, bound, skew, True), shares(amount, rows * top, bound, skew, False)
    places = jnp.arange(amount)

    def named(lengths, turn):
        used = int((lengths > 0).sum())
        fixed = max(1, used // 4)
        shifted = fixed + (places - fixed + turn * (used - fixed)) % max(1, amount - fixed)
        return jnp.zeros((amount,), jnp.int32).at[order[jnp.where(places < fixed, places, shifted)]].set(jnp.asarray(lengths, jnp.int32))

    lengths = jnp.where(number % 4 == 0, named(packed, number // 4), named(ordinary, number - number // 4 - 1))
    mixed = jax.random.permutation(jax.random.fold_in(own, 3), amount)
    giver, sink = mixed[0:amount // 2 * 2:2], mixed[1:amount // 2 * 2:2]
    margin = jnp.minimum(lengths[giver] - 1, bound - lengths[sink]) // 2
    margin = jnp.where((giver == order[0]) | (sink == order[0]) | (lengths[sink] == 0), 0, jnp.maximum(margin, 0))
    shifted = jax.random.randint(jax.random.fold_in(own, 4), (amount // 2,), 0, 1 << 20) % (margin + 1)
    lengths = lengths.at[giver].add(-shifted).at[sink].add(shifted)
    labels = jnp.searchsorted(jnp.cumsum(lengths), jnp.arange(rows * top), side="right").astype(jnp.int32)
    table = labels.reshape(top, rows).T
    table = table[jax.random.permutation(jax.random.fold_in(own, 1), rows)]
    turn = jax.random.randint(jax.random.fold_in(own, 2), (rows, 1), 0, top)
    return jnp.take_along_axis(table, (jnp.arange(top)[None, :] + turn) % top, axis=1)


def shares(count, total, bound, skew, full):
    portions = [(1 << 20) // math.isqrt(rank ** skew) + 1 for rank in range(1, count + 1)]
    largest = bound if full else min(bound, max(-(-total // count), total * portions[0] // sum(portions)))
    least = 1 if total - largest >= count - 1 else 0
    holding, surplus = [largest] + [least] * (count - 1), total - largest - least * (count - 1)
    while surplus > 0:
        free = [i for i in range(1, count) if holding[i] < largest] or [i for i in range(1, count) if holding[i] < bound]
        mass, remaining = sum([portions[i] for i in free]), surplus
        for i in free:
            more = min(bound - holding[i], max(1, remaining * portions[i] // mass), surplus)
            holding[i] = holding[i] + more
            surplus = surplus - more
    return np.array(holding)


def centred(stream_key, shape, deviation, most, pieces=(), held_as=jnp.bfloat16):
    level = block_levels(stream_key, shape, pieces, -0.22, 0.18) if pieces else 1.0
    entries = jax.random.normal(stream_key, shape, jnp.float32) * deviation * level
    return jnp.minimum(jnp.maximum(entries, -most), most).astype(held_as)


def setup_inputs(seed: int = 0) -> dict:
    keys = jax.random.split(jax.random.key(seed), 6)
    factor_blocks = centred(keys[0], (NBLK, NAUX, TT), TV ** -0.5, 1.25, ((0, 32), (1, 16)))
    amplitudes = centred(keys[1], (NBLK, NPAIR, TT), NAUX ** -0.5, 0.15625, ((0, 32), (1, 16)))
    residual_in = centred(keys[2], (NBLK, NPAIR, TT), 1.0, 6.0, ((0, 32), (1, 16)), jnp.float32)
    task_owners_keys = jax.random.split(jax.random.fold_in(keys[3], 1), NTASK // N_PAIR)
    task_owners_turns = jax.random.permutation(jax.random.fold_in(keys[3], 3), NTASK // N_PAIR)
    task_owners = jax.vmap(lambda own, number: shared_out(jax.random.fold_in(keys[3], 2), own, number, N_PAIR, N_TASK, 3, MOST, 2))(task_owners_keys, task_owners_turns).reshape((NTASK, 3))
    task_local = with_ends(jax.random.randint(keys[4], (NTASK, 4), 0, BLK_DEV), jax.random.fold_in(keys[4], 1), 0, BLK_DEV - 1).astype(jnp.int32)
    return {"factor_blocks": factor_blocks, "amplitudes": amplitudes, "residual_in": residual_in, "task_owners": task_owners, "task_local": task_local}


def reference(factor_blocks, amplitudes, residual_in, task_owners, task_local):
    task_total = task_owners.shape[0]
    columns = (jnp.arange(task_total, dtype=jnp.int32) // N_PAIR).astype(jnp.int32)
    row_ids = (task_owners[:, 0] * BLK_DEV + task_local[:, 0]).astype(jnp.int32)
    col_ids = (task_owners[:, 1] * BLK_DEV + task_local[:, 1]).astype(jnp.int32)
    amp_ids = (task_owners[:, 2] * BLK_DEV + task_local[:, 2]).astype(jnp.int32)
    out_ids = (columns * BLK_DEV + task_local[:, 3]).astype(jnp.int32)

    def one_task(accumulated, indices):
        row_id, col_id, amp_id, out_id = indices
        row_factor = lax.dynamic_index_in_dim(factor_blocks, row_id, 0, keepdims=False)
        col_factor = lax.dynamic_index_in_dim(factor_blocks, col_id, 0, keepdims=False)
        amp_block = lax.dynamic_index_in_dim(amplitudes, amp_id, 0, keepdims=False)
        integral_tile = jnp.dot(row_factor.T, col_factor, preferred_element_type=jnp.float32).astype(jnp.bfloat16)
        ladder = jnp.einsum('icd,acbd->iab', amp_block.reshape(NPAIR, TV, TV).astype(jnp.float32), integral_tile.reshape(TV, TV, TV, TV).astype(jnp.float32))
        ladder = ladder.astype(jnp.bfloat16).reshape(NPAIR, TT)
        current = lax.dynamic_index_in_dim(accumulated, out_id, 0, keepdims=False)
        updated = current + ladder.astype(accumulated.dtype)
        accumulated = lax.dynamic_update_index_in_dim(accumulated, updated, out_id, 0)
        return accumulated, None

    result, ignored = lax.scan(one_task, residual_in, (row_ids, col_ids, amp_ids, out_ids))
    return result
```

```python
import functools

import jax
import jax.numpy as jnp
from jax import lax
from jax.experimental import pallas as pl
from jax.experimental.pallas import tpu as pltpu
from jax.sharding import PartitionSpec as P

TV = 25
TT = 625
CH = 5
LN = 128
WIDE = CH * LN
STAGGER = 2.0
MESH = pl.DeviceIdType.MESH


def spread_matrix(swapped):
    k = lax.broadcasted_iota(jnp.int32, (TT, WIDE), 0)
    lane = lax.broadcasted_iota(jnp.int32, (TT, WIDE), 1)
    x = (k * 5243) >> 17
    y = k - x * TV
    if swapped:
        x, y = y, x
    group = (x * 13) >> 6
    target = group * LN + (x - group * 5) * TV + y
    return (lane == target).astype(jnp.float32).astype(jnp.bfloat16)


def kernel(
    base_ref, out_local_ref, factor_ref, amp_ref, residual_ref, out_ref,
    tiles, g0, g1, g2, g3, g4, s0, s1, s2, s3, s4, r0, r1, r2, r3, r4,
    v_ref, q_ref, w_ref, l_send, l_recv,
    spread_send, spread_recv, ring_send, ring_recv, plane_send, plane_recv, back_send, back_recv,
):
    gathered = (g0, g1, g2, g3, g4)
    sends = (s0, s1, s2, s3, s4)
    recvs = (r0, r1, r2, r3, r4)
    pair = lax.axis_index("pair")
    task = lax.axis_index("task")
    y, zl = pair // 4, pair % 4
    zh, x, core = task // 8, (task // 2) % 4, task % 2
    z = zh * 4 + zl

    def place(py, pz, px, pc):
        return {"pair": py * 4 + pz % 4, "task": ((pz // 4) * 4 + px) * 2 + pc}

    right = place(y, (z + 1) % 16, x, core)
    left = place(y, (z + 15) % 16, x, core)

    def plane_peer(n):
        return (y + n // 8) % 4, (x + (n // 2) % 4) % 4, (core + n % 2) % 2

    def column_peer(n):
        return (y + n // 4) % 4, (zl + n % 4) % 4

    barrier = pltpu.get_barrier_semaphore()

    @pl.loop(1, 32)
    def _(n):
        py, px, pc = plane_peer(n)
        pl.semaphore_signal(barrier, inc=1, device_id=place(py, z, px, pc), device_id_type=MESH)

    @pl.loop(1, 16)
    def _(n):
        py, pz = column_peer(n)
        pl.semaphore_signal(barrier, inc=1, device_id=place(py, zh * 4 + pz, x, core), device_id_type=MESH)

    pl.semaphore_signal(barrier, inc=1, device_id=right, device_id_type=MESH)
    pl.semaphore_signal(barrier, inc=1, device_id=left, device_id_type=MESH)

    spread = spread_matrix(False)
    for loc in range(2):
        rows = jnp.dot(factor_ref[loc], spread, preferred_element_type=jnp.float32).astype(jnp.bfloat16)
        for tile in range(6):
            for ch in range(CH):
                tiles[tile, ch, loc] = rows[tile * 16 : tile * 16 + 16, ch * LN : (ch + 1) * LN]
    swap = spread_matrix(True)
    for loc in range(2):
        rows = jnp.dot(amp_ref[loc], swap, preferred_element_type=jnp.float32).astype(jnp.bfloat16)
        for tile in range(2):
            for ch in range(CH):
                tiles[6 + tile, ch, loc] = rows[tile * 16 : tile * 16 + 16, ch * LN : (ch + 1) * LN]

    pl.semaphore_wait(barrier, 48)

    for ch in range(CH):
        for n in range(8):
            px, pc = (x + n // 2) % 4, (core + n % 2) % 2
            src = tiles.at[((px + 7 - zl) % 4) * 2 + pc, ch]
            dst = gathered[ch].at[pl.ds(z * 16 + (x * 2 + core) * 2, 2)]
            if n == 0:
                pltpu.make_async_copy(src, dst, spread_recv.at[ch]).start()
            else:
                pltpu.make_async_remote_copy(
                    src, dst, spread_send, spread_recv.at[ch], device_id=place(y, z, px, pc), device_id_type=MESH
                ).start()

    def slot(ch, zz, half=None):
        if half is None:
            return gathered[ch].at[pl.ds(zz * 16, 16)]
        return gathered[ch].at[pl.ds(zz * 16 + half * 8, 8)]

    def ring_copy(ch, side, step, zz):
        ref = slot(ch, zz, None if step < 7 else side)
        return pltpu.make_async_remote_copy(
            ref, ref, ring_send.at[ch], ring_recv.at[(ch * 2 + side) * 8 + step],
            device_id=right if side == 0 else left, device_id_type=MESH,
        )

    def ring(ch, step):
        if step == 0:
            own = slot(ch, z)
            pltpu.make_async_copy(own, own, spread_recv.at[ch]).wait()
        for side in range(2):
            zz = (z + 16 - step) % 16 if side == 0 else (z + step) % 16
            if step > 0:
                ring_copy(ch, side, step - 1, zz).wait_recv()
            if step < 8:
                ring_copy(ch, side, step, zz).start()

    def plane(ch):
        got, send, recv = gathered[ch], sends[ch], recvs[ch]

        @pl.loop(0, 32)
        def _(n):
            py, px, pc = plane_peer(n)
            k = ((zh * 4 + px) * 2 + pc) * 16 + py * 4 + zl
            row, col, amp = base_ref[k * 3], base_ref[k * 3 + 1], base_ref[k * 3 + 2]
            for r in range(3):
                at = ((x + 1 + r) % 4) * 16
                send[n, r] = got[row + at]
                send[n, 3 + r] = got[col + at]
            send[n, 6] = got[amp + x * 16]

        dst = recv.at[(y * 4 + x) * 2 + core]
        pltpu.make_async_copy(send.at[0], dst, plane_recv.at[ch]).start()

        @pl.loop(1, 32)
        def _(n):
            py, px, pc = plane_peer(n)
            pltpu.make_async_remote_copy(
                send.at[n], dst, plane_send.at[ch], plane_recv.at[ch],
                device_id=place(py, z, px, pc), device_id_type=MESH,
            ).start()

    def integrals(ch):
        recv = recvs[ch]
        pltpu.make_async_copy(recv, recv, plane_recv.at[ch]).wait()

        def rows_of(c, kb, first):
            return recvs[c][pl.ds(kb * 8, 8), first : first + 3].reshape(384, LN)

        for kb in range(4):
            row = rows_of(ch, kb, 0)
            cols = [rows_of(c, kb, 3) for c in range(ch + 1)]
            part = lax.dot_general(
                row, jnp.concatenate(cols, axis=1), (((0,), (0,)), ((), ())), preferred_element_type=jnp.float32
            )
            at = (slice(ch * LN, (ch + 1) * LN), slice(0, (ch + 1) * LN))
            v_ref[at] = part if kb == 0 else v_ref[at] + part
            if ch:
                before = jnp.concatenate([rows_of(c, kb, 0) for c in range(ch)], axis=1)
                part = lax.dot_general(
                    before, cols[-1], (((0,), (0,)), ((), ())), preferred_element_type=jnp.float32
                )
                at = (slice(0, ch * LN), slice(ch * LN, (ch + 1) * LN))
                v_ref[at] = part if kb == 0 else v_ref[at] + part

    events = []
    for ch in range(CH):
        for step in range(9):
            events.append((step + ch * STAGGER, ch, functools.partial(ring, ch, step)))
        events.append((8 + ch * STAGGER + 0.01, ch, functools.partial(plane, ch)))
        events.append((8 + ch * STAGGER + 5.0, ch, functools.partial(integrals, ch)))
    for _, _, event in sorted(events, key=lambda e: (e[0], e[1])):
        event()

    r = lax.broadcasted_iota(jnp.int32, (TV * 32, WIDE), 0)
    lane = lax.broadcasted_iota(jnp.int32, (TV * 32, WIDE), 1)
    d, b = r >> 5, r & 31
    group = (b * 13) >> 6
    target = jnp.where(b < TV, group * LN + (b - group * 5) * TV + d, -1)
    turn = (lane == target).astype(jnp.float32).astype(jnp.bfloat16)
    turned = lax.dot_general(
        turn, v_ref[...].astype(jnp.bfloat16), (((1,), (1,)), ((), ())), preferred_element_type=jnp.float32
    )
    q_ref[...] = turned.reshape(TV, 32, WIDE)

    lanes = lax.broadcasted_iota(jnp.int32, (32, LN), 1)

    @pl.loop(0, CH)
    def _(i):
        lane_i = pl.ds(pl.multiple_of(i * LN, LN), LN)
        for g in range(CH):
            src = [q_ref[g * 5 + dd, :, lane_i] for dd in range(5)]
            for aa in range(5):
                acc = jnp.zeros((32, LN), jnp.float32)
                for dd in range(5):
                    shift = ((dd - aa) * TV) % LN
                    moved = pltpu.roll(src[dd], shift, 1) if shift else src[dd]
                    acc = jnp.where((lanes >= dd * TV) & (lanes < (dd + 1) * TV), moved, acc)
                count = TV if aa < 4 else 28
                w_ref[i, aa * TV : aa * TV + count, g * LN : (g + 1) * LN] = acc[:count]

    amps = jnp.concatenate([recvs[c][:, 6].reshape(512, LN) for c in range(CH)], axis=1)
    for i in range(CH):
        ladder = lax.dot_general(
            amps, w_ref[i].astype(jnp.bfloat16), (((1,), (1,)), ((), ())), preferred_element_type=jnp.float32
        )
        l_send[:, i] = ladder.astype(jnp.bfloat16).reshape(16, 32, LN)

    l_dst = l_recv.at[pair]
    pltpu.make_async_copy(l_send.at[pair], l_dst, back_recv).start()

    @pl.loop(1, 16)
    def _(n):
        py, pz = column_peer(n)
        pltpu.make_async_remote_copy(
            l_send.at[py * 4 + pz], l_dst, back_send, back_recv,
            device_id=place(py, zh * 4 + pz, x, core), device_id_type=MESH,
        ).start()

    part = tiles.at[pl.ds(0, 7)]
    pltpu.make_async_copy(part, part, spread_send).wait()
    for ch in range(CH):
        part = gathered[ch].at[pl.ds(0, 240)]
        pltpu.make_async_copy(part, part, ring_send.at[ch]).wait()
        part = sends[ch].at[pl.ds(0, 31)]
        pltpu.make_async_copy(part, part, plane_send.at[ch]).wait()

    pltpu.make_async_copy(l_recv, l_recv, back_recv).wait()
    for i in range(CH):
        sums = [jnp.zeros((32, LN), jnp.float32) for _ in range(2)]
        for src in range(16):
            tile = l_recv[src, i].astype(jnp.float32)
            here = out_local_ref[task * 16 + src]
            sums = [sums[loc] + jnp.where(here == loc, tile, 0.0) for loc in range(2)]
        for loc in range(2):
            v_ref[loc * 32 : loc * 32 + 32, i * LN : (i + 1) * LN] = sums[loc]
    for loc in range(2):
        total = v_ref[loc * 32 : loc * 32 + 32, :]
        joined = jnp.concatenate([total[:, i * LN : i * LN + 125] for i in range(CH)], axis=1)
        out_ref[loc] = residual_ref[loc] + joined
    part = l_send.at[pl.ds(0, 15)]
    pltpu.make_async_copy(part, part, back_send).wait()


def per_device(factor_blocks, amplitudes, residual_in, task_owners, task_local):
    ids = task_owners * 2 + task_local[:, :3]
    base = ((ids // 16) * 64 + ids % 16).reshape(-1)
    out_local = task_local[:, 3]
    vmem = pl.BlockSpec(memory_space=pltpu.VMEM)
    smem = pl.BlockSpec(memory_space=pltpu.SMEM)
    bf16, f32 = jnp.bfloat16, jnp.float32
    dma = pltpu.SemaphoreType.DMA
    return pl.pallas_call(
        kernel,
        out_shape=jax.ShapeDtypeStruct(residual_in.shape, residual_in.dtype),
        in_specs=[smem, smem, vmem, vmem, vmem],
        out_specs=vmem,
        scratch_shapes=[pltpu.VMEM((8, CH, 2, 16, LN), bf16)]
        + [pltpu.VMEM((256, 16, LN), bf16)] * CH
        + [pltpu.VMEM((32, 7, 16, LN), bf16)] * (2 * CH)
        + [
            pltpu.VMEM((WIDE, WIDE), f32),
            pltpu.VMEM((TV, 32, WIDE), f32),
            pltpu.VMEM((CH, LN, WIDE), f32),
            pltpu.VMEM((16, CH, 32, LN), bf16),
            pltpu.VMEM((16, CH, 32, LN), bf16),
            dma,
            dma((CH,)),
            dma((CH,)),
            dma((CH * 16,)),
            dma((CH,)),
            dma((CH,)),
            dma,
            dma,
        ],
        compiler_params=pltpu.CompilerParams(collective_id=0, has_side_effects=True),
    )(base, out_local, factor_blocks, amplitudes, residual_in)


def solution(mesh):
    placed = (P("task", "pair", None), P("task", "pair", None), P("task", "pair", None), P(), P())
    return jax.shard_map(
        per_device, mesh=mesh, in_specs=placed, out_specs=P("task", "pair", None), check_vma=False
    )
```

```python
import functools

import jax
import jax.numpy as jnp
from jax import lax
from jax.experimental import pallas as pl
from jax.experimental.pallas import tpu as pltpu
from jax.sharding import PartitionSpec as P

TV = 25
TT = 625
CH = 5
LN = 128
WIDE = CH * LN
MESH = pl.DeviceIdType.MESH
HALF_US = 0.72
HOP_US = 2.2
READY_US = 0.7


def ring_order():
    ready = {(ch, half): ch * READY_US for ch in range(CH) for half in range(2)}
    step = {key: 0 for key in ready}
    order, now = [], 0.0
    while ready:
        now = max(now, min(ready.values()))
        key = min((k for k in ready if ready[k] <= now), key=lambda k: (24 + 8.3 * k[0] - (8 - step[k]) * 2.9, k))
        order.append((now, key, step[key]))
        at = step[key]
        step[key] += 1
        if at == 8:
            del ready[key]
            continue
        now += HALF_US if at < 7 else HALF_US / 2
        ready[key] = now + HOP_US
    return order


def swap_matrix():
    k = lax.broadcasted_iota(jnp.int32, (TT, WIDE), 0)
    lane = lax.broadcasted_iota(jnp.int32, (TT, WIDE), 1)
    c = (k * 5243) >> 17
    d = k - c * TV
    group = (d * 13) >> 6
    target = group * LN + (d - group * 5) * TV + c
    return (lane == target).astype(jnp.float32).astype(jnp.bfloat16)


def turn_matrix():
    r = lax.broadcasted_iota(jnp.int32, (TV * 32, WIDE), 0)
    lane = lax.broadcasted_iota(jnp.int32, (TV * 32, WIDE), 1)
    d, b = r >> 5, r & 31
    group = (b * 13) >> 6
    target = jnp.where(b < TV, group * LN + (b - group * 5) * TV + d, -1)
    return (lane == target).astype(jnp.float32).astype(jnp.bfloat16)


def kernel(
    owners_ref, local_ref, factor_hbm, amp_hbm, residual_hbm, out_ref,
    factor_ref, amp_ref, residual_ref, base_ref, turn_ref,
    tiles, g0, g1, g2, g3, g4, s0, s1, s2, s3, s4, r0, r1, r2, r3, r4,
    v_ref, q_ref, w_ref, l_send, l_recv, sum_ref,
    load_sem, spread_send, spread_recv, ring_send, ring_recv, plane_send, plane_recv, back_send, back_recv,
):
    gathered = (g0, g1, g2, g3, g4)
    sends = (s0, s1, s2, s3, s4)
    recvs = (r0, r1, r2, r3, r4)
    loads = [
        pltpu.make_async_copy(src, dst, load_sem.at[i])
        for i, (src, dst) in enumerate(
            ((factor_hbm, factor_ref), (amp_hbm, amp_ref), (residual_hbm, residual_ref))
        )
    ]
    for load in loads:
        load.start()

    pair = lax.axis_index("pair")
    task = lax.axis_index("task")
    y, zl = pair // 4, pair % 4
    zh, x, core = task // 8, (task // 2) % 4, task % 2
    z = zh * 4 + zl

    def place(py, pz, px, pc):
        return {"pair": py * 4 + pz % 4, "task": ((pz // 4) * 4 + px) * 2 + pc}

    right = place(y, (z + 1) % 16, x, core)
    left = place(y, (z + 15) % 16, x, core)

    def plane_peer(n):
        n = (n * 5) % 32
        return (y + n // 8) % 4, (x + (n // 2) % 4) % 4, (core + n % 2) % 2

    def column_peer(n):
        return (y + n // 4) % 4, (zl + n % 4) % 4

    barrier = pltpu.get_barrier_semaphore()

    @pl.loop(1, 32)
    def _(n):
        py, px, pc = plane_peer(n)
        pl.semaphore_signal(barrier, inc=1, device_id=place(py, z, px, pc), device_id_type=MESH)

    @pl.loop(1, 16)
    def _(n):
        py, pz = column_peer(n)
        pl.semaphore_signal(barrier, inc=1, device_id=place(py, zh * 4 + pz, x, core), device_id_type=MESH)

    pl.semaphore_signal(barrier, inc=1, device_id=right, device_id_type=MESH)
    pl.semaphore_signal(barrier, inc=1, device_id=left, device_id_type=MESH)

    swap = swap_matrix()
    loads[0].wait()
    for loc in range(2):
        for ch in range(CH):
            rows = factor_ref[loc, :, ch * 125 : ch * 125 + 125]
            rows = jnp.concatenate([rows, jnp.zeros((96, 3), jnp.bfloat16)], axis=1)
            tiles[0:6, ch, loc] = rows.reshape(6, 16, LN)
    loads[1].wait()
    for loc in range(2):
        rows = jnp.dot(amp_ref[loc], swap, preferred_element_type=jnp.float32).astype(jnp.bfloat16)
        for ch in range(CH):
            tiles[6:8, ch, loc] = rows[:, ch * LN : (ch + 1) * LN].reshape(2, 16, LN)

    pl.semaphore_wait(barrier, 48)

    for ch in range(CH):
        for n in range(8):
            px, pc = (x + n // 2) % 4, (core + n % 2) % 2
            src = tiles.at[((px + 7 - zl) % 4) * 2 + pc, ch]
            dst = gathered[ch].at[pl.ds(z * 16 + (x * 2 + core) * 2, 2)]
            if n == 0:
                pltpu.make_async_copy(src, dst, spread_recv.at[ch]).start()
            else:
                pltpu.make_async_remote_copy(
                    src, dst, spread_send, spread_recv.at[ch], device_id=place(y, z, px, pc), device_id_type=MESH
                ).start()

    @pl.loop(0, 32)
    def _(n):
        py, px, pc = plane_peer(n)
        k = ((zh * 4 + px) * 2 + pc) * 16 + py * 4 + zl
        for i in range(3):
            m = owners_ref[i, k] * 2 + local_ref[i, k]
            base_ref[n * 3 + i] = (m // 16) * 64 + m % 16

    def half_slot(ch, zz, half):
        return gathered[ch].at[pl.ds(zz * 16 + half * 8, 8)]

    def ring_copy(ch, half, side, step, zz):
        ref = half_slot(ch, zz, half)
        return pltpu.make_async_remote_copy(
            ref, ref, ring_send.at[ch], ring_recv.at[((ch * 2 + half) * 2 + side) * 8 + step],
            device_id=right if side == 0 else left, device_id_type=MESH,
        )

    spread_done = [False] * CH

    def ring(ch, half, step):
        if step == 0 and not spread_done[ch]:
            own = gathered[ch].at[pl.ds(z * 16, 16)]
            pltpu.make_async_copy(own, own, spread_recv.at[ch]).wait()
            spread_done[ch] = True
        for side in range(2):
            zz = (z + 16 - step) % 16 if side == 0 else (z + step) % 16
            if 0 < step < 8 or (step == 8 and side == half):
                ring_copy(ch, half, side, step - 1, zz).wait_recv()
            if step < 7 or (step == 7 and side == half):
                ring_copy(ch, half, side, step, zz).start()

    def plane(ch):
        got, send, recv = gathered[ch], sends[ch], recvs[ch]
        dst = recv.at[(y * 4 + x) * 2 + core]

        @pl.loop(0, 32)
        def _(n):
            row, col, amp = base_ref[n * 3], base_ref[n * 3 + 1], base_ref[n * 3 + 2]
            for r in range(3):
                at = ((x + 1 + r) % 4) * 16
                send[n, r] = got[row + at]
                send[n, 3 + r] = got[col + at]
            send[n, 6] = got[amp + x * 16]

        pltpu.make_async_copy(send.at[0], dst, plane_recv.at[ch]).start()

        @pl.loop(1, 32)
        def _(n):
            py, px, pc = plane_peer(n)
            pltpu.make_async_remote_copy(
                send.at[n], dst, plane_send.at[ch], plane_recv.at[ch],
                device_id=place(py, z, px, pc), device_id_type=MESH,
            ).start()

    def integrals(ch, kb):
        recv = recvs[ch]
        if kb == 0:
            pltpu.make_async_copy(recv, recv, plane_recv.at[ch]).wait()

        def rows_of(c, first):
            return recvs[c][pl.ds(kb * 8, 8), first : first + 3].reshape(384, LN)

        row = rows_of(ch, 0)
        cols = [rows_of(c, 3) for c in range(ch + 1)]
        part = lax.dot_general(
            row, jnp.concatenate(cols, axis=1), (((0,), (0,)), ((), ())), preferred_element_type=jnp.float32
        )
        at = (slice(ch * LN, (ch + 1) * LN), slice(0, (ch + 1) * LN))
        v_ref[at] = part if kb == 0 else v_ref[at] + part
        if ch:
            before = jnp.concatenate([rows_of(c, 0) for c in range(ch)], axis=1)
            part = lax.dot_general(before, cols[-1], (((0,), (0,)), ((), ())), preferred_element_type=jnp.float32)
            at = (slice(0, ch * LN), slice(ch * LN, (ch + 1) * LN))
            v_ref[at] = part if kb == 0 else v_ref[at] + part

    def make_turn():
        turn_ref[...] = turn_matrix()

    PLANE_US = 10.0
    order = ring_order()
    events = [(t, functools.partial(ring, ch, half, step)) for t, (ch, half), step in order]
    free = 0.0
    for ch in range(CH):
        done = max(t for t, (c, _), step in order if c == ch and step == 8)
        events.append((done + 1e-4, functools.partial(plane, ch)))
        free = max(free, done) + PLANE_US
        for kb in range(4):
            events.append((free + 4.0 + kb * 1.5, functools.partial(integrals, ch, kb)))
    events.append((8.0, make_turn))
    for _, event in sorted(events, key=lambda e: e[0]):
        event()

    amps = jnp.concatenate([recvs[c][:, 6].reshape(512, LN) for c in range(CH)], axis=1)
    lanes = lax.broadcasted_iota(jnp.int32, (32, LN), 1)

    @pl.loop(0, CH)
    def _(i):
        part = v_ref[pl.ds(pl.multiple_of(i * LN, LN), LN), :].astype(jnp.bfloat16)
        turned = lax.dot_general(turn_ref[...], part, (((1,), (1,)), ((), ())), preferred_element_type=jnp.float32)
        q_ref[...] = turned.reshape(TV, 32, LN)
        for g in range(CH):
            src = [q_ref[g * 5 + dd] for dd in range(5)]
            for aa in range(5):
                acc = jnp.zeros((32, LN), jnp.float32)
                for dd in range(5):
                    shift = ((dd - aa) * TV) % LN
                    moved = pltpu.roll(src[dd], shift, 1) if shift else src[dd]
                    acc = jnp.where((lanes >= dd * TV) & (lanes < (dd + 1) * TV), moved, acc)
                count = TV if aa < 4 else 28
                w_ref[aa * TV : aa * TV + count, g * LN : (g + 1) * LN] = acc[:count]
        ladder = lax.dot_general(
            amps, w_ref[...].astype(jnp.bfloat16), (((1,), (1,)), ((), ())), preferred_element_type=jnp.float32
        )
        l_send[i] = ladder.astype(jnp.bfloat16).reshape(16, 32, LN)
        dst = l_recv.at[i, pair]
        pltpu.make_async_copy(l_send.at[i, pair], dst, back_recv.at[i]).start()

        @pl.loop(1, 16)
        def _(n):
            py, pz = column_peer(n)
            pltpu.make_async_remote_copy(
                l_send.at[i, py * 4 + pz], dst, back_send, back_recv.at[i],
                device_id=place(py, zh * 4 + pz, x, core), device_id_type=MESH,
            ).start()

    part = tiles.at[pl.ds(0, 7)]
    pltpu.make_async_copy(part, part, spread_send).wait()
    for ch in range(CH):
        part = gathered[ch].at[pl.ds(0, 240)]
        pltpu.make_async_copy(part, part, ring_send.at[ch]).wait()
        part = sends[ch].at[pl.ds(0, 31)]
        pltpu.make_async_copy(part, part, plane_send.at[ch]).wait()

    loads[2].wait()
    for i in range(CH):
        pltpu.make_async_copy(l_recv.at[i], l_recv.at[i], back_recv.at[i]).wait()
        sums = [jnp.zeros((32, LN), jnp.float32) for _ in range(2)]
        for src in range(16):
            tile = l_recv[i, src].astype(jnp.float32)
            here = local_ref[3, task * 16 + src]
            sums = [sums[loc] + jnp.where(here == loc, tile, 0.0) for loc in range(2)]
        for loc in range(2):
            sum_ref[loc, :, i * LN : (i + 1) * LN] = sums[loc]
    for loc in range(2):
        joined = jnp.concatenate([sum_ref[loc, :, i * LN : i * LN + 125] for i in range(CH)], axis=1)
        out_ref[loc] = residual_ref[loc] + joined
    part = l_send.at[:, pl.ds(0, 15)]
    pltpu.make_async_copy(part, part, back_send).wait()


def per_device(factor_blocks, amplitudes, residual_in, task_owners, task_local):
    vmem = pl.BlockSpec(memory_space=pltpu.VMEM)
    smem = pl.BlockSpec(memory_space=pltpu.SMEM)
    hbm = pl.BlockSpec(memory_space=pl.ANY)
    bf16, f32 = jnp.bfloat16, jnp.float32
    dma = pltpu.SemaphoreType.DMA
    return pl.pallas_call(
        kernel,
        out_shape=jax.ShapeDtypeStruct(residual_in.shape, residual_in.dtype),
        in_specs=[smem, smem, hbm, hbm, hbm],
        out_specs=vmem,
        scratch_shapes=[
            pltpu.VMEM(factor_blocks.shape, bf16),
            pltpu.VMEM(amplitudes.shape, bf16),
            pltpu.VMEM(residual_in.shape, f32),
            pltpu.SMEM((96,), jnp.int32),
            pltpu.VMEM((TV * 32, WIDE), bf16),
            pltpu.VMEM((8, CH, 2, 16, LN), bf16),
        ]
        + [pltpu.VMEM((256, 16, LN), bf16)] * CH
        + [pltpu.VMEM((32, 7, 16, LN), bf16)] * (2 * CH)
        + [
            pltpu.VMEM((WIDE, WIDE), f32),
            pltpu.VMEM((TV, 32, LN), f32),
            pltpu.VMEM((LN, WIDE), f32),
            pltpu.VMEM((CH, 16, 32, LN), bf16),
            pltpu.VMEM((CH, 16, 32, LN), bf16),
            pltpu.VMEM((2, 32, WIDE), f32),
            dma((3,)),
            dma,
            dma((CH,)),
            dma((CH,)),
            dma((CH * 32,)),
            dma((CH,)),
            dma((CH,)),
            dma,
            dma((CH,)),
        ],
        compiler_params=pltpu.CompilerParams(collective_id=0, has_side_effects=True),
    )(task_owners.T, task_local.T, factor_blocks, amplitudes, residual_in)


def solution(mesh):
    placed = (P("task", "pair", None), P("task", "pair", None), P("task", "pair", None), P(), P())
    return jax.shard_map(
        per_device, mesh=mesh, in_specs=placed, out_specs=P("task", "pair", None), check_vma=False
    )
```

```python
import functools

import jax
import jax.numpy as jnp
from jax import lax
from jax.experimental import pallas as pl
from jax.experimental.pallas import tpu as pltpu
from jax.sharding import PartitionSpec as P

TV = 25
TT = 625
CH = 5
LN = 128
WIDE = CH * LN
MESH = pl.DeviceIdType.MESH
HALF_US = 0.72
HOP_US = 2.4
READY_US = 0.7
DUE_US = (15.4, 24.9, 38.1, 47.5, 49.5)


def ring_order():
    ready = {(ch, half): ch * READY_US for ch in range(CH) for half in range(2)}
    step = {key: 0 for key in ready}
    order, now = [], 0.0
    while ready:
        now = max(now, min(ready.values()))
        key = min((k for k in ready if ready[k] <= now), key=lambda k: (DUE_US[k[0]] - (8 - step[k]) * 2.9, k))
        order.append((now, key, step[key]))
        at = step[key]
        step[key] += 1
        if at == 8:
            del ready[key]
            continue
        now += HALF_US if at < 7 else HALF_US / 2
        ready[key] = now + HOP_US
    return order


def swap_matrix():
    k = lax.broadcasted_iota(jnp.int32, (TT, WIDE), 0)
    lane = lax.broadcasted_iota(jnp.int32, (TT, WIDE), 1)
    c = (k * 5243) >> 17
    d = k - c * TV
    group = (d * 13) >> 6
    target = group * LN + (d - group * 5) * TV + c
    return (lane == target).astype(jnp.float32).astype(jnp.bfloat16)


def turn_matrix():
    r = lax.broadcasted_iota(jnp.int32, (TV * 8, LN), 0)
    lane = lax.broadcasted_iota(jnp.int32, (TV * 8, LN), 1)
    d, b = r >> 3, r & 7
    target = jnp.where(b < 5, b * TV + d, -1)
    return (lane == target).astype(jnp.float32).astype(jnp.bfloat16)


def kernel(
    owners_ref, local_ref, factor_hbm, amp_hbm, residual_hbm, out_ref,
    factor_ref, amp_ref, residual_ref, base_ref, turn_ref, tiles, *more,
):
    gathered = [list(more[ch * 4 : ch * 4 + 4]) for ch in range(CH)]
    sends, recvs = more[20:25], more[25:30]
    v_ref, w_ref, l_send, l_recv, m_send, m_recv, sum_ref = more[30:37]
    (
        load_sem, spread_send, spread_recv, ring_send, ring_recv,
        plane_send, plane_recv, back_send, back_recv, last_send, last_recv,
    ) = more[37:]
    loads = [
        pltpu.make_async_copy(src, dst, load_sem.at[i])
        for i, (src, dst) in enumerate(
            ((factor_hbm, factor_ref), (amp_hbm, amp_ref), (residual_hbm, residual_ref))
        )
    ]
    for load in loads:
        load.start()

    pair = lax.axis_index("pair")
    task = lax.axis_index("task")
    y, zl = pair // 4, pair % 4
    zh, x, core = task // 8, (task // 2) % 4, task % 2
    z = zh * 4 + zl

    def place(py, pz, px, pc):
        return {"pair": py * 4 + pz % 4, "task": ((pz // 4) * 4 + px) * 2 + pc}

    right = place(y, (z + 1) % 16, x, core)
    left = place(y, (z + 15) % 16, x, core)

    def plane_peer(n):
        n = (n * 5) % 32
        return (y + n // 8) % 4, (x + (n // 2) % 4) % 4, (core + n % 2) % 2

    barrier = pltpu.get_barrier_semaphore()

    @pl.loop(1, 32)
    def _(n):
        py, px, pc = plane_peer(n)
        pl.semaphore_signal(barrier, inc=1, device_id=place(py, z, px, pc), device_id_type=MESH)

    for n in range(1, 4):
        pl.semaphore_signal(
            barrier, inc=1, device_id=place(y, zh * 4 + (zl + n) % 4, x, core), device_id_type=MESH
        )
    pl.semaphore_signal(barrier, inc=1, device_id=right, device_id_type=MESH)
    pl.semaphore_signal(barrier, inc=1, device_id=left, device_id_type=MESH)

    swap = swap_matrix()
    loads[0].wait()
    for loc in range(2):
        for ch in range(CH):
            rows = factor_ref[loc, :, ch * 125 : ch * 125 + 125]
            rows = jnp.concatenate([rows, jnp.zeros((96, 3), jnp.bfloat16)], axis=1)
            tiles[0:6, ch, loc] = rows.reshape(6, 16, LN)
    loads[1].wait()
    for loc in range(2):
        rows = jnp.dot(amp_ref[loc], swap, preferred_element_type=jnp.float32).astype(jnp.bfloat16)
        for ch in range(CH):
            tiles[6:8, ch, loc] = rows[:, ch * LN : (ch + 1) * LN].reshape(2, 16, LN)

    pl.semaphore_wait(barrier, 36)

    for ch in range(CH):
        for n in range(8):
            px, pc = (x + n // 2) % 4, (core + n % 2) % 2
            src = tiles.at[((px + 7 - zl) % 4) * 2 + pc, ch]
            dst = gathered[ch][0].at[pl.ds(zh * 16 + (x * 2 + core) * 2, 2)]
            if n == 0:
                pltpu.make_async_copy(src, dst, spread_recv.at[ch]).start()
            else:
                pltpu.make_async_remote_copy(
                    src, dst, spread_send, spread_recv.at[ch], device_id=place(y, z, px, pc), device_id_type=MESH
                ).start()

    @pl.loop(0, 32)
    def _(n):
        py, px, pc = plane_peer(n)
        k = ((zh * 4 + px) * 2 + pc) * 16 + py * 4 + zl
        for i in range(3):
            base_ref[n * 3 + i] = owners_ref[i, k] * 2 + local_ref[i, k]

    def ring_copy(ch, half, side, step, zz):
        way = -1 if side == 0 else 1
        at = pl.ds((zz // 4) * 16 + half * 8, 8)
        return pltpu.make_async_remote_copy(
            gathered[ch][(way * step) % 4].at[at], gathered[ch][(way * (step + 1)) % 4].at[at],
            ring_send.at[ch], ring_recv.at[((ch * 2 + half) * 2 + side) * 8 + step],
            device_id=right if side == 0 else left, device_id_type=MESH,
        )

    spread_done = [False] * CH

    def ring(ch, half, step):
        if step == 0 and not spread_done[ch]:
            own = gathered[ch][0].at[pl.ds(zh * 16, 16)]
            pltpu.make_async_copy(own, own, spread_recv.at[ch]).wait()
            spread_done[ch] = True
        for side in range(2):
            zz = (z + 16 - step) % 16 if side == 0 else (z + step) % 16
            if 0 < step < 8 or (step == 8 and side == half):
                ring_copy(ch, half, side, step - 1, zz).wait_recv()
            if step < 7 or (step == 7 and side == half):
                ring_copy(ch, half, side, step, zz).start()

    def plane(ch, classes):
        send, recv = sends[ch], recvs[ch]
        seat = (y * 4 + x) * 2 + core

        @pl.loop(0, 32)
        def _(n):
            row, col, amp = base_ref[n * 3], base_ref[n * 3 + 1], base_ref[n * 3 + 2]
            for q in classes:
                r = (q + zl - x + 4) % 4
                tile = ((r + 3) % 4) * 2
                send[n, tile] = gathered[ch][q][jnp.where(r == 0, amp, row)]
                send[n, tile + 1] = gathered[ch][q][col]

        def out(first, count):
            for n in range(1, 32):
                py, px, pc = plane_peer(n)
                pltpu.make_async_remote_copy(
                    send.at[n, pl.ds(first, count)], recv.at[seat, pl.ds(first, count)],
                    plane_send.at[ch], plane_recv.at[ch],
                    device_id=place(py, z, px, pc), device_id_type=MESH,
                ).start()

        for q in classes:
            r = (q + zl - x + 4) % 4

            @pl.when(r == 0)
            def _():
                out(6, 1)

            @pl.when(r != 0)
            def _():
                out(((r + 3) % 4) * 2, 2)

        if 0 in classes:
            pltpu.make_async_copy(send.at[0, pl.ds(0, 7)], recv.at[seat], plane_recv.at[ch]).start()

    def integrals(ch, kb):
        recv = recvs[ch]
        if kb == 0:
            pltpu.make_async_copy(recv, recv, plane_recv.at[ch]).wait()

        def rows_of(c, first):
            both = recvs[c][pl.ds(kb * 8, 8), 0:6].reshape(8, 3, 2, 16, LN)
            return both[:, :, first].reshape(384, LN)

        row = rows_of(ch, 0)
        cols = [rows_of(c, 1) for c in range(ch + 1)]
        part = lax.dot_general(
            row, jnp.concatenate(cols, axis=1), (((0,), (0,)), ((), ())), preferred_element_type=jnp.float32
        )
        at = (slice(ch * LN, (ch + 1) * LN), slice(0, (ch + 1) * LN))
        v_ref[at] = part if kb == 0 else v_ref[at] + part
        if ch:
            before = jnp.concatenate([rows_of(c, 0) for c in range(ch)], axis=1)
            part = lax.dot_general(before, cols[-1], (((0,), (0,)), ((), ())), preferred_element_type=jnp.float32)
            at = (slice(0, ch * LN), slice(ch * LN, (ch + 1) * LN))
            v_ref[at] = part if kb == 0 else v_ref[at] + part

    def make_turn():
        turn_ref[...] = turn_matrix()
        w_ref[...] = jnp.zeros(w_ref.shape, jnp.float32)

    lanes = lax.broadcasted_iota(jnp.int32, (8, LN), 1)

    def relay(i, j):
        part = v_ref[i * LN : (i + 1) * LN, j * LN : (j + 1) * LN].astype(jnp.bfloat16)
        turned = lax.dot_general(turn_ref[...], part, (((1,), (1,)), ((), ())), preferred_element_type=jnp.float32)
        turned = turned.reshape(TV, 8, LN)
        for g in range(CH):
            for aa in range(5):
                acc = jnp.zeros((8, LN), jnp.float32)
                for dd in range(5):
                    moved = turned[g * 5 + dd]
                    shift = ((dd - aa) * TV) % LN
                    if shift:
                        moved = pltpu.roll(moved, shift, 1)
                    acc = jnp.where((lanes >= dd * TV) & (lanes < (dd + 1) * TV), moved, acc)
                first = aa * TV + j * 5
                w_ref[i, first : first + 5, g * LN : (g + 1) * LN] = acc[:5]

    PLANE_US = 10.0
    order = ring_order()
    events = [(t, functools.partial(ring, ch, half, step)) for t, (ch, half), step in order]
    free = 0.0
    for ch in range(CH):
        reached = {n: max(t for t, (c, _), step in order if c == ch and step == n) for n in (6, 7, 8)}
        for n, classes in ((6, (2,)), (7, (1, 3)), (8, (0,))):
            events.append((reached[n] + 1e-4, functools.partial(plane, ch, classes)))
        free = max(free, reached[8]) + PLANE_US
        for kb in range(4):
            events.append((free + 4.0 + kb * 1.5, functools.partial(integrals, ch, kb)))
        if ch < CH - 1:
            for n in range(ch + 1):
                events.append((free + 9.5 + n * 0.1, functools.partial(relay, ch, n)))
                if n < ch:
                    events.append((free + 9.55 + n * 0.1, functools.partial(relay, n, ch)))
    events.append((8.0, make_turn))
    for _, event in sorted(events, key=lambda e: e[0]):
        event()

    amps = jnp.concatenate([recvs[c][:, 6].reshape(512, LN) for c in range(CH)], axis=1)

    def ladder(i):
        for j in range(CH):
            if max(i, j) == CH - 1:
                relay(i, j)
        tiles_i = lax.dot_general(
            amps, w_ref[i].astype(jnp.bfloat16), (((1,), (1,)), ((), ())), preferred_element_type=jnp.float32
        )
        l_send[i] = tiles_i.astype(jnp.bfloat16).reshape(16, 32, LN)
        dst = l_recv.at[i, y]
        for n in (1, 3, 2):
            py = (y + n) % 4
            pltpu.make_async_remote_copy(
                l_send.at[i, pl.ds(py * 4, 4)], dst, back_send, back_recv.at[i],
                device_id=place(py, z, x, core), device_id_type=MESH,
            ).start()
        pltpu.make_async_copy(l_send.at[i, pl.ds(y * 4, 4)], dst, back_recv.at[i]).start()

    def select(local, tile, loc):
        return jnp.where(local == loc, tile, 0.0)

    def fold(i):
        pltpu.make_async_copy(l_recv.at[i], l_recv.at[i], back_recv.at[i]).wait()
        locals_i = [local_ref[3, task * 16 + src * 4 + zl] for src in range(4)]
        for pz in range(4):
            got = [l_recv[i, src, pz].astype(jnp.float32) for src in range(4)]
            for loc in range(2):
                total = select(locals_i[0], got[0], loc)
                for src in range(1, 4):
                    total = total + select(locals_i[src], got[src], loc)
                m_send[i, pz, loc] = total.astype(jnp.bfloat16)
        dst = m_recv.at[i, zl]
        for n in (2, 1, 3):
            pz = (zl + n) % 4
            pltpu.make_async_remote_copy(
                m_send.at[i, pz], dst, last_send, last_recv.at[i],
                device_id=place(y, zh * 4 + pz, x, core), device_id_type=MESH,
            ).start()
        pltpu.make_async_copy(m_send.at[i, zl], dst, last_recv.at[i]).start()

    for i in range(CH + 3):
        if i < CH:
            ladder(i)
        if i >= 3:
            fold(i - 3)

    part = tiles.at[pl.ds(0, 7)]
    pltpu.make_async_copy(part, part, spread_send).wait()
    for ch in range(CH):
        part = sends[ch].at[pl.ds(0, 30)]
        pltpu.make_async_copy(part, part, ring_send.at[ch]).wait()
        part = recvs[ch].at[pl.ds(0, 31)]
        pltpu.make_async_copy(part, part, plane_send.at[ch]).wait()

    loads[2].wait()
    for i in range(CH):
        pltpu.make_async_copy(m_recv.at[i], m_recv.at[i], last_recv.at[i]).wait()
        for loc in range(2):
            total = m_recv[i, 0, loc].astype(jnp.float32)
            for src in range(1, 4):
                total = total + m_recv[i, src, loc].astype(jnp.float32)
            sum_ref[loc, :, i * LN : (i + 1) * LN] = total
    for loc in range(2):
        joined = jnp.concatenate([sum_ref[loc, :, i * LN : i * LN + 125] for i in range(CH)], axis=1)
        out_ref[loc] = residual_ref[loc] + joined
    part = l_send.at[:, pl.ds(0, 12)]
    pltpu.make_async_copy(part, part, back_send).wait()
    part = m_send.at[:, pl.ds(0, 3)]
    pltpu.make_async_copy(part, part, last_send).wait()


def per_device(factor_blocks, amplitudes, residual_in, task_owners, task_local):
    vmem = pl.BlockSpec(memory_space=pltpu.VMEM)
    smem = pl.BlockSpec(memory_space=pltpu.SMEM)
    hbm = pl.BlockSpec(memory_space=pl.ANY)
    bf16, f32 = jnp.bfloat16, jnp.float32
    dma = pltpu.SemaphoreType.DMA
    return pl.pallas_call(
        kernel,
        out_shape=jax.ShapeDtypeStruct(residual_in.shape, residual_in.dtype),
        in_specs=[smem, smem, hbm, hbm, hbm],
        out_specs=vmem,
        scratch_shapes=[
            pltpu.VMEM(factor_blocks.shape, bf16),
            pltpu.VMEM(amplitudes.shape, bf16),
            pltpu.VMEM(residual_in.shape, f32),
            pltpu.SMEM((96,), jnp.int32),
            pltpu.VMEM((TV * 8, LN), bf16),
            pltpu.VMEM((8, CH, 2, 16, LN), bf16),
        ]
        + [pltpu.VMEM((64, 16, LN), bf16)] * (4 * CH)
        + [pltpu.VMEM((32, 8, 16, LN), bf16)] * CH
        + [pltpu.VMEM((32, 7, 16, LN), bf16)] * CH
        + [
            pltpu.VMEM((WIDE, WIDE), f32),
            pltpu.VMEM((CH, LN, WIDE), f32),
            pltpu.VMEM((CH, 16, 32, LN), bf16),
            pltpu.VMEM((CH, 4, 4, 32, LN), bf16),
            pltpu.VMEM((CH, 4, 2, 32, LN), bf16),
            pltpu.VMEM((CH, 4, 2, 32, LN), bf16),
            pltpu.VMEM((2, 32, WIDE), f32),
            dma((3,)),
            dma,
            dma((CH,)),
            dma((CH,)),
            dma((CH * 32,)),
            dma((CH,)),
            dma((CH,)),
            dma,
            dma((CH,)),
            dma,
            dma((CH,)),
        ],
        compiler_params=pltpu.CompilerParams(collective_id=0, has_side_effects=True),
    )(task_owners.T, task_local.T, factor_blocks, amplitudes, residual_in)


def solution(mesh):
    placed = (P("task", "pair", None), P("task", "pair", None), P("task", "pair", None), P(), P())
    return jax.shard_map(
        per_device, mesh=mesh, in_specs=placed, out_specs=P("task", "pair", None), check_vma=False
    )
```

```python
import functools

import jax
import jax.numpy as jnp
from jax import lax
from jax.experimental import pallas as pl
from jax.experimental.pallas import tpu as pltpu
from jax.sharding import PartitionSpec as P

TV = 25
TT = 625
CH = 5
LN = 128
WIDE = CH * LN
MESH = pl.DeviceIdType.MESH
HALF_US = 0.72
HOP_US = 2.4
READY_US = 0.7
DUE_US = (15.4, 24.9, 38.1, 47.5, 49.5)


def ring_order():
    ready = {(ch, half): ch * READY_US for ch in range(CH) for half in range(2)}
    step = {key: 0 for key in ready}
    order, now = [], 0.0
    while ready:
        now = max(now, min(ready.values()))
        key = min((k for k in ready if ready[k] <= now), key=lambda k: (DUE_US[k[0]] - (8 - step[k]) * 2.9, k))
        order.append((now, key, step[key]))
        at = step[key]
        step[key] += 1
        if at == 8:
            del ready[key]
            continue
        now += HALF_US if at < 7 else HALF_US / 2
        ready[key] = now + HOP_US
    return order


def swap_matrix():
    k = lax.broadcasted_iota(jnp.int32, (TT, WIDE), 0)
    lane = lax.broadcasted_iota(jnp.int32, (TT, WIDE), 1)
    c = (k * 5243) >> 17
    d = k - c * TV
    group = (d * 13) >> 6
    target = group * LN + (d - group * 5) * TV + c
    return (lane == target).astype(jnp.float32).astype(jnp.bfloat16)


def turn_matrix():
    r = lax.broadcasted_iota(jnp.int32, (TV * 8, LN), 0)
    lane = lax.broadcasted_iota(jnp.int32, (TV * 8, LN), 1)
    d, b = r >> 3, r & 7
    target = jnp.where(b < 5, b * TV + d, -1)
    return (lane == target).astype(jnp.float32).astype(jnp.bfloat16)


def kernel(
    owners_ref, local_ref, factor_hbm, amp_hbm, residual_hbm, out_ref,
    factor_ref, amp_ref, residual_ref, base_ref, turn_ref, tiles, *more,
):
    gathered = [list(more[ch * 4 : ch * 4 + 4]) for ch in range(CH)]
    sends, recvs = more[20:25], more[25:30]
    v_ref, w_ref, l_send, l_recv, m_send, m_recv, sum_ref = more[30:37]
    (
        load_sem, spread_send, spread_recv, ring_send, ring_recv,
        plane_send, plane_recv, back_send, back_recv, last_send, last_recv,
    ) = more[37:]
    loads = [
        pltpu.make_async_copy(src, dst, load_sem.at[i])
        for i, (src, dst) in enumerate(
            ((factor_hbm, factor_ref), (amp_hbm, amp_ref), (residual_hbm, residual_ref))
        )
    ]
    for load in loads:
        load.start()

    pair = lax.axis_index("pair")
    task = lax.axis_index("task")
    y, zl = pair // 4, pair % 4
    zh, x, core = task // 8, (task // 2) % 4, task % 2
    z = zh * 4 + zl

    def place(py, pz, px, pc):
        return {"pair": py * 4 + pz % 4, "task": ((pz // 4) * 4 + px) * 2 + pc}

    right = place(y, (z + 1) % 16, x, core)
    left = place(y, (z + 15) % 16, x, core)

    def plane_peer(n):
        n = (n * 13) % 32
        return (y + n // 8) % 4, (x + (n // 2) % 4) % 4, (core + n % 2) % 2

    barrier = pltpu.get_barrier_semaphore()

    @pl.loop(1, 32)
    def _(n):
        py, px, pc = plane_peer(n)
        pl.semaphore_signal(barrier, inc=1, device_id=place(py, z, px, pc), device_id_type=MESH)

    for n in range(1, 4):
        pl.semaphore_signal(
            barrier, inc=1, device_id=place(y, zh * 4 + (zl + n) % 4, x, core), device_id_type=MESH
        )
    pl.semaphore_signal(barrier, inc=1, device_id=right, device_id_type=MESH)
    pl.semaphore_signal(barrier, inc=1, device_id=left, device_id_type=MESH)

    swap = swap_matrix()
    loads[0].wait()
    for loc in range(2):
        for ch in range(CH):
            rows = factor_ref[loc, :, ch * 125 : ch * 125 + 125]
            rows = jnp.concatenate([rows, jnp.zeros((96, 3), jnp.bfloat16)], axis=1)
            tiles[0:6, ch, loc] = rows.reshape(6, 16, LN)
    loads[1].wait()
    for loc in range(2):
        rows = jnp.dot(amp_ref[loc], swap, preferred_element_type=jnp.float32).astype(jnp.bfloat16)
        for ch in range(CH):
            tiles[6:8, ch, loc] = rows[:, ch * LN : (ch + 1) * LN].reshape(2, 16, LN)

    pl.semaphore_wait(barrier, 36)

    for ch in range(CH):
        for n in range(8):
            px, pc = (x + n // 2) % 4, (core + n % 2) % 2
            src = tiles.at[((px + 7 - zl) % 4) * 2 + pc, ch]
            dst = gathered[ch][0].at[pl.ds(zh * 16 + (x * 2 + core) * 2, 2)]
            if n == 0:
                pltpu.make_async_copy(src, dst, spread_recv.at[ch]).start()
            else:
                pltpu.make_async_remote_copy(
                    src, dst, spread_send, spread_recv.at[ch], device_id=place(y, z, px, pc), device_id_type=MESH
                ).start()

    @pl.loop(0, 32)
    def _(n):
        py, px, pc = plane_peer(n)
        k = ((zh * 4 + px) * 2 + pc) * 16 + py * 4 + zl
        for i in range(3):
            base_ref[n * 3 + i] = owners_ref[i, k] * 2 + local_ref[i, k]

    def ring_copy(ch, half, side, step, zz):
        way = -1 if side == 0 else 1
        at = pl.ds((zz // 4) * 16 + half * 8, 8)
        return pltpu.make_async_remote_copy(
            gathered[ch][(way * step) % 4].at[at], gathered[ch][(way * (step + 1)) % 4].at[at],
            ring_send.at[ch], ring_recv.at[((ch * 2 + half) * 2 + side) * 8 + step],
            device_id=right if side == 0 else left, device_id_type=MESH,
        )

    spread_done = [False] * CH

    def ring(ch, half, step):
        if step == 0 and not spread_done[ch]:
            own = gathered[ch][0].at[pl.ds(zh * 16, 16)]
            pltpu.make_async_copy(own, own, spread_recv.at[ch]).wait()
            spread_done[ch] = True
        for side in range(2):
            zz = (z + 16 - step) % 16 if side == 0 else (z + step) % 16
            if 0 < step < 8 or (step == 8 and side == half):
                ring_copy(ch, half, side, step - 1, zz).wait_recv()
            if step < 7 or (step == 7 and side == half):
                ring_copy(ch, half, side, step, zz).start()

    def plane(ch, classes):
        send, recv = sends[ch], recvs[ch]
        seat = (y * 4 + x) * 2 + core

        @pl.loop(0, 4)
        def _(part):
            held = []
            for n in range(8):
                n = part * 8 + n
                row, col, amp = base_ref[n * 3], base_ref[n * 3 + 1], base_ref[n * 3 + 2]
                for q in classes:
                    r = (q + zl - x + 4) % 4
                    tile = ((r + 3) % 4) * 2
                    held.append((n, tile, gathered[ch][q][jnp.where(r == 0, amp, row)], gathered[ch][q][col]))
            for n, tile, first, second in held:
                send[n, tile] = first
                send[n, tile + 1] = second

        def out(first, count):
            for n in range(1, 32):
                py, px, pc = plane_peer(n)
                pltpu.make_async_remote_copy(
                    send.at[n, pl.ds(first, count)], recv.at[seat, pl.ds(first, count)],
                    plane_send.at[ch], plane_recv.at[ch],
                    device_id=place(py, z, px, pc), device_id_type=MESH,
                ).start()

        for q in classes:
            r = (q + zl - x + 4) % 4

            @pl.when(r == 0)
            def _():
                out(6, 1)

            @pl.when(r != 0)
            def _():
                out(((r + 3) % 4) * 2, 2)

        if 0 in classes:
            pltpu.make_async_copy(send.at[0, pl.ds(0, 7)], recv.at[seat], plane_recv.at[ch]).start()

    def integrals(ch, kb):
        recv = recvs[ch]
        if kb == 0:
            pltpu.make_async_copy(recv, recv, plane_recv.at[ch]).wait()

        def rows_of(c, first):
            both = recvs[c][pl.ds(kb * 8, 8), 0:6].reshape(8, 3, 2, 16, LN)
            return both[:, :, first].reshape(384, LN)

        row = rows_of(ch, 0)
        cols = [rows_of(c, 1) for c in range(ch + 1)]
        part = lax.dot_general(
            row, jnp.concatenate(cols, axis=1), (((0,), (0,)), ((), ())), preferred_element_type=jnp.float32
        )
        at = (slice(ch * LN, (ch + 1) * LN), slice(0, (ch + 1) * LN))
        v_ref[at] = part if kb == 0 else v_ref[at] + part
        if ch:
            before = jnp.concatenate([rows_of(c, 0) for c in range(ch)], axis=1)
            part = lax.dot_general(before, cols[-1], (((0,), (0,)), ((), ())), preferred_element_type=jnp.float32)
            at = (slice(0, ch * LN), slice(ch * LN, (ch + 1) * LN))
            v_ref[at] = part if kb == 0 else v_ref[at] + part

    def make_turn():
        turn_ref[...] = turn_matrix()
        w_ref[...] = jnp.zeros(w_ref.shape, jnp.float32)

    lanes = lax.broadcasted_iota(jnp.int32, (8, LN), 1)

    def relay(i, j):
        part = v_ref[i * LN : (i + 1) * LN, j * LN : (j + 1) * LN].astype(jnp.bfloat16)
        turned = lax.dot_general(turn_ref[...], part, (((1,), (1,)), ((), ())), preferred_element_type=jnp.float32)
        turned = turned.reshape(TV, 8, LN)
        for g in range(CH):
            for aa in range(5):
                acc = jnp.zeros((8, LN), jnp.float32)
                for dd in range(5):
                    moved = turned[g * 5 + dd]
                    shift = ((dd - aa) * TV) % LN
                    if shift:
                        moved = pltpu.roll(moved, shift, 1)
                    acc = jnp.where((lanes >= dd * TV) & (lanes < (dd + 1) * TV), moved, acc)
                first = aa * TV + j * 5
                w_ref[i, first : first + 5, g * LN : (g + 1) * LN] = acc[:5]

    PLANE_US = 10.0
    order = ring_order()
    events = [(t, functools.partial(ring, ch, half, step)) for t, (ch, half), step in order]
    free = 0.0
    for ch in range(CH):
        reached = {n: max(t for t, (c, _), step in order if c == ch and step == n) for n in (6, 7, 8)}
        for n, classes in ((6, (2,)), (7, (1, 3)), (8, (0,))):
            events.append((reached[n] + 1e-4, functools.partial(plane, ch, classes)))
        free = max(free, reached[8]) + PLANE_US
        for kb in range(4):
            events.append((free + 4.0 + kb * 1.5, functools.partial(integrals, ch, kb)))
        if ch < CH - 1:
            for n in range(ch + 1):
                events.append((free + 9.5 + n * 0.1, functools.partial(relay, ch, n)))
                if n < ch:
                    events.append((free + 9.55 + n * 0.1, functools.partial(relay, n, ch)))
    events.append((8.0, make_turn))
    for _, event in sorted(events, key=lambda e: e[0]):
        event()

    amps = jnp.concatenate([recvs[c][:, 6].reshape(512, LN) for c in range(CH)], axis=1)

    def ladder(i):
        for j in range(CH):
            if max(i, j) == CH - 1:
                relay(i, j)
        tiles_i = lax.dot_general(
            amps, w_ref[i].astype(jnp.bfloat16), (((1,), (1,)), ((), ())), preferred_element_type=jnp.float32
        )
        l_send[i] = tiles_i.astype(jnp.bfloat16).reshape(16, 32, LN)
        dst = l_recv.at[i, y]
        for n in (1, 3, 2):
            py = (y + n) % 4
            pltpu.make_async_remote_copy(
                l_send.at[i, pl.ds(py * 4, 4)], dst, back_send, back_recv.at[i],
                device_id=place(py, z, x, core), device_id_type=MESH,
            ).start()
        pltpu.make_async_copy(l_send.at[i, pl.ds(y * 4, 4)], dst, back_recv.at[i]).start()

    def select(local, tile, loc):
        return jnp.where(local == loc, tile, 0.0)

    def fold(i):
        pltpu.make_async_copy(l_recv.at[i], l_recv.at[i], back_recv.at[i]).wait()
        locals_i = [local_ref[3, task * 16 + src * 4 + zl] for src in range(4)]
        for pz in range(4):
            got = [l_recv[i, src, pz].astype(jnp.float32) for src in range(4)]
            for loc in range(2):
                total = select(locals_i[0], got[0], loc)
                for src in range(1, 4):
                    total = total + select(locals_i[src], got[src], loc)
                m_send[i, pz, loc] = total.astype(jnp.bfloat16)
        dst = m_recv.at[i, zl]
        for n in (2, 1, 3):
            pz = (zl + n) % 4
            pltpu.make_async_remote_copy(
                m_send.at[i, pz], dst, last_send, last_recv.at[i],
                device_id=place(y, zh * 4 + pz, x, core), device_id_type=MESH,
            ).start()
        pltpu.make_async_copy(m_send.at[i, zl], dst, last_recv.at[i]).start()

    for i in range(CH + 3):
        if i < CH:
            ladder(i)
        if i >= 3:
            fold(i - 3)

    part = tiles.at[pl.ds(0, 7)]
    pltpu.make_async_copy(part, part, spread_send).wait()
    for ch in range(CH):
        part = sends[ch].at[pl.ds(0, 30)]
        pltpu.make_async_copy(part, part, ring_send.at[ch]).wait()
        part = recvs[ch].at[pl.ds(0, 31)]
        pltpu.make_async_copy(part, part, plane_send.at[ch]).wait()

    loads[2].wait()
    for i in range(CH):
        pltpu.make_async_copy(m_recv.at[i], m_recv.at[i], last_recv.at[i]).wait()
        for loc in range(2):
            total = m_recv[i, 0, loc].astype(jnp.float32)
            for src in range(1, 4):
                total = total + m_recv[i, src, loc].astype(jnp.float32)
            sum_ref[loc, :, i * LN : (i + 1) * LN] = total
    for loc in range(2):
        joined = jnp.concatenate([sum_ref[loc, :, i * LN : i * LN + 125] for i in range(CH)], axis=1)
        out_ref[loc] = residual_ref[loc] + joined
    part = l_send.at[:, pl.ds(0, 12)]
    pltpu.make_async_copy(part, part, back_send).wait()
    part = m_send.at[:, pl.ds(0, 3)]
    pltpu.make_async_copy(part, part, last_send).wait()


def per_device(factor_blocks, amplitudes, residual_in, task_owners, task_local):
    vmem = pl.BlockSpec(memory_space=pltpu.VMEM)
    smem = pl.BlockSpec(memory_space=pltpu.SMEM)
    hbm = pl.BlockSpec(memory_space=pl.ANY)
    bf16, f32 = jnp.bfloat16, jnp.float32
    dma = pltpu.SemaphoreType.DMA
    return pl.pallas_call(
        kernel,
        out_shape=jax.ShapeDtypeStruct(residual_in.shape, residual_in.dtype),
        in_specs=[smem, smem, hbm, hbm, hbm],
        out_specs=vmem,
        scratch_shapes=[
            pltpu.VMEM(factor_blocks.shape, bf16),
            pltpu.VMEM(amplitudes.shape, bf16),
            pltpu.VMEM(residual_in.shape, f32),
            pltpu.SMEM((96,), jnp.int32),
            pltpu.VMEM((TV * 8, LN), bf16),
            pltpu.VMEM((8, CH, 2, 16, LN), bf16),
        ]
        + [pltpu.VMEM((64, 16, LN), bf16)] * (4 * CH)
        + [pltpu.VMEM((32, 8, 16, LN), bf16)] * CH
        + [pltpu.VMEM((32, 7, 16, LN), bf16)] * CH
        + [
            pltpu.VMEM((WIDE, WIDE), f32),
            pltpu.VMEM((CH, LN, WIDE), f32),
            pltpu.VMEM((CH, 16, 32, LN), bf16),
            pltpu.VMEM((CH, 4, 4, 32, LN), bf16),
            pltpu.VMEM((CH, 4, 2, 32, LN), bf16),
            pltpu.VMEM((CH, 4, 2, 32, LN), bf16),
            pltpu.VMEM((2, 32, WIDE), f32),
            dma((3,)),
            dma,
            dma((CH,)),
            dma((CH,)),
            dma((CH * 32,)),
            dma((CH,)),
            dma((CH,)),
            dma,
            dma((CH,)),
            dma,
            dma((CH,)),
        ],
        compiler_params=pltpu.CompilerParams(collective_id=0, has_side_effects=True),
    )(task_owners.T, task_local.T, factor_blocks, amplitudes, residual_in)


def solution(mesh):
    placed = (P("task", "pair", None), P("task", "pair", None), P("task", "pair", None), P(), P())
    return jax.shard_map(
        per_device, mesh=mesh, in_specs=placed, out_specs=P("task", "pair", None), check_vma=False
    )
```
